32 devices in a mesh: seq: 8 (over y, x, core), head: 4 (over z).
Axes of the slice: x: 2, y: 2, z: 4, core: 2. Of those that a mesh axis runs over, the one named last changes fastest.
Arguments:
- tokens: float32 [2048, 1024], P('seq'), may hold values from -6 to 6
- doc_start: int32 [2048], P('seq'), may hold values from 0 to 1, as said below
- cotangent: float32 [2048, 1024], P('seq'), may hold values from -6 to 6
- norm_in: float32 [1024], replicated, may hold values from 0.5 to 1.5
- w_in: float32 [1024, 8, 768], P('seq', 'head'), may hold values from -0.1875 to 0.1875
- w_gates: float32 [1024, 2, 8], P('seq', None, 'head'), may hold values from -0.1875 to 0.1875
- conv_w: float32 [4, 8, 512], P(None, 'head'), may hold values from -3 to 3
- decay: float32 [2, 8], P(None, 'head')
- norm_out: float32 [256], replicated, may hold values from 0.5 to 1.5
- w_out: float32 [8, 256, 1024], P('head', None, 'seq'), may hold values from -0.125 to 0.125
- norm_ffn: float32 [1024], replicated, may hold values from 0.5 to 1.5
- w_up: float32 [1024, 2, 2816], P('seq', None, 'head'), may hold values from -0.1875 to 0.1875
- w_down: float32 [2816, 1024], P('head', 'seq'), may hold values from -0.109375 to 0.109375
- moment_norm_in: float32 [1024], replicated, may hold values from -80 to 80
- moment_w_in: float32 [1024, 8, 768], P('seq', 'head'), may hold values from -80 to 80
- moment_w_gates: float32 [1024, 2, 8], P('seq', None, 'head'), may hold values from -80 to 80
- moment_conv_w: float32 [4, 8, 512], P(None, 'head'), may hold values from -80 to 80
- moment_decay: float32 [2, 8], P(None, 'head'), may hold values from -80 to 80
- moment_norm_out: float32 [256], replicated, may hold values from -80 to 80
- moment_w_out: float32 [8, 256, 1024], P('head', None, 'seq'), may hold values from -80 to 80
- moment_norm_ffn: float32 [1024], replicated, may hold values from -80 to 80
- moment_w_up: float32 [1024, 2, 2816], P('seq', None, 'head'), may hold values from -80 to 80
- moment_w_down: float32 [2816, 1024], P('head', 'seq'), may hold values from -80 to 80
Outputs:
- output: float32 [2048, 1024], P('seq')
- grad_tokens: float32 [2048, 1024], P('seq')
- grad_norm_in: float32 [1024], replicated
- grad_w_in: float32 [1024, 8, 768], P('seq', 'head')
- grad_w_gates: float32 [1024, 2, 8], P('seq', None, 'head')
- grad_conv_w: float32 [4, 8, 512], P(None, 'head')
- grad_decay: float32 [2, 8], P(None, 'head')
- grad_norm_out: float32 [256], replicated
- grad_w_out: float32 [8, 256, 1024], P('head', None, 'seq')
- grad_norm_ffn: float32 [1024], replicated
- grad_w_up: float32 [1024, 2, 2816], P('seq', None, 'head')
- grad_w_down: float32 [2816, 1024], P('head', 'seq')
- new_norm_in: float32 [1024], replicated
- new_w_in: float32 [1024, 8, 768], P('seq', 'head')
- new_w_gates: float32 [1024, 2, 8], P('seq', None, 'head')
- new_conv_w: float32 [4, 8, 512], P(None, 'head')
- new_decay: float32 [2, 8], P(None, 'head')
- new_norm_out: float32 [256], replicated
- new_w_out: float32 [8, 256, 1024], P('head', None, 'seq')
- new_norm_ffn: float32 [1024], replicated
- new_w_up: float32 [1024, 2, 2816], P('seq', None, 'head')
- new_w_down: float32 [2816, 1024], P('head', 'seq')
- new_moment_norm_in: float32 [1024], replicated
- new_moment_w_in: float32 [1024, 8, 768], P('seq', 'head')
- new_moment_w_gates: float32 [1024, 2, 8], P('seq', None, 'head')
- new_moment_conv_w: float32 [4, 8, 512], P(None, 'head')
- new_moment_decay: float32 [2, 8], P(None, 'head')
- new_moment_norm_out: float32 [256], replicated
- new_moment_w_out: float32 [8, 256, 1024], P('head', None, 'seq')
- new_moment_norm_ffn: float32 [1024], replicated
- new_moment_w_up: float32 [1024, 2, 2816], P('seq', None, 'head')
- new_moment_w_down: float32 [2816, 1024], P('head', 'seq')
The draws below stay inside these ranges and needn't reach their ends.
Inputs may be any that keep to these rules, and one draw needn't show every extreme that they name: `doc_start`: exactly two entries are 1: one at a position from 1 to 1023, one from 1024 to 2047.
All inputs are finite; a program needn't handle non-finite values.
Results may differ from the reference program's by a relative error of at most 0.023.
Values may be sent and summed in bfloat16 or wider, within the bound.
A program may use at most 128 MiB of HBM per device.

```python
import functools
import math
import jax
import jax.numpy as jnp
from jax import lax

D = 1024
H = 8
KEY_SIZE = 128
VALUE_SIZE = 256
FF = 2816
CONV = 4
BLOCK_TOKENS = 64
FG = 352
QKVG = 768
CONV_CH = 512
TOKENS = 2048


def draw_doc_start(key, part):
    first, second = jax.random.split(jax.random.fold_in(key, 11))
    half = TOKENS // 2
    place_one = jax.random.randint(first, (), 1, half)
    place_two = jax.random.randint(second, (), half, TOKENS)
    positions = jnp.arange(TOKENS)
    return ((positions == place_one) | (positions == place_two)).astype(jnp.int32)


def draw_decay(key, part):
    scale_key, bias_key = jax.random.split(jax.random.fold_in(key, 23))
    lowest = math.log(0.5 / TOKENS)
    highest = math.log(0.05)
    log_scale = jax.random.uniform(scale_key, (H,), jnp.float32, lowest, highest)
    biases = jax.random.uniform(bias_key, (H,), jnp.float32, -0.5, 0.5)
    return jnp.stack([log_scale, biases])


def block_levels(rng, shape, cuts, least, largest):
    loudness = 1.0
    for axis_at, shards_of in cuts:
        steps = jax.random.uniform(jax.random.fold_in(jax.random.fold_in(rng, 6), axis_at), (shards_of,), jnp.float32, least / len(cuts), largest / len(cuts))
        loudness = loudness * jnp.repeat(jnp.exp(steps), shape[axis_at] // shards_of).reshape((-1,) + (1,) * (len(shape) - 1 - axis_at))
    return loudness


def noise(own_key, dims, scale, most, cuts=(), held_as=jnp.bfloat16):
    loudness = block_levels(own_key, dims, cuts, -0.22, 0.18) if cuts else 1.0
    drawn = jax.random.normal(own_key, dims, jnp.float32) * scale * loudness
    return jnp.minimum(jnp.maximum(drawn, -most), most).astype(held_as)


def setup_inputs(seed: int = 0) -> dict:
    keys = jax.random.split(jax.random.key(seed), 24)
    tokens = noise(keys[0], (TOKENS, D), 1.0, 6.0, ((0, 8),), jnp.float32)
    doc_start = draw_doc_start(jax.random.fold_in(keys[23], 71), 0)
    cotangent = noise(keys[2], (TOKENS, D), 1.0, 6.0, ((0, 8),), jnp.float32)
    norm_in = jnp.clip(1.0 + 0.1 * jax.random.normal(keys[3], (D,), jnp.float32), 0.5, 1.5)
    w_in = noise(keys[4], (D, H, QKVG), D ** -0.5, 0.1875, ((0, 8), (1, 4)), jnp.float32)
    w_gates = noise(keys[5], (D, 2, H), D ** -0.5, 0.1875, ((0, 8), (2, 4)), jnp.float32)
    conv_w = noise(keys[6], (CONV, H, CONV_CH), CONV ** -0.5, 3.0, ((1, 4),), jnp.float32)
    decay = draw_decay(jax.random.fold_in(keys[23], 71), 0)
    norm_out = jnp.clip(1.0 + 0.1 * jax.random.normal(keys[8], (VALUE_SIZE,), jnp.float32), 0.5, 1.5)
    w_out = noise(keys[9], (H, VALUE_SIZE, D), (H * VALUE_SIZE) ** -0.5, 0.125, ((0, 4), (2, 8)), jnp.float32)
    norm_ffn = jnp.clip(1.0 + 0.1 * jax.random.normal(keys[10], (D,), jnp.float32), 0.5, 1.5)
    w_up = noise(keys[11], (D, 2, FF), D ** -0.5, 0.1875, ((0, 8), (2, 4)), jnp.float32)
    w_down = noise(keys[12], (FF, D), FF ** -0.5, 0.109375, ((0, 4), (1, 8)), jnp.float32)
    moment_norm_in = noise(keys[13], (D,), (0.3 * TOKENS ** 0.5), 80.0, (), jnp.float32)
    moment_w_in = noise(keys[14], (D, H, QKVG), (0.3 * TOKENS ** 0.5), 80.0, ((0, 8), (1, 4)), jnp.float32)
    moment_w_gates = noise(keys[15], (D, 2, H), (0.3 * TOKENS ** 0.5), 80.0, ((0, 8), (2, 4)), jnp.float32)
    moment_conv_w = noise(keys[16], (CONV, H, CONV_CH), (0.3 * TOKENS ** 0.5), 80.0, ((1, 4),), jnp.float32)
    moment_decay = noise(keys[17], (2, H), (0.3 * TOKENS ** 0.5), 80.0, ((1, 4),), jnp.float32)
    moment_norm_out = noise(keys[18], (VALUE_SIZE,), (0.3 * TOKENS ** 0.5), 80.0, (), jnp.float32)
    moment_w_out = noise(keys[19], (H, VALUE_SIZE, D), (0.3 * TOKENS ** 0.5), 80.0, ((0, 4), (2, 8)), jnp.float32)
    moment_norm_ffn = noise(keys[20], (D,), (0.3 * TOKENS ** 0.5), 80.0, (), jnp.float32)
    moment_w_up = noise(keys[21], (D, 2, FF), (0.3 * TOKENS ** 0.5), 80.0, ((0, 8), (2, 4)), jnp.float32)
    moment_w_down = noise(keys[22], (FF, D), (0.3 * TOKENS ** 0.5), 80.0, ((0, 4), (1, 8)), jnp.float32)
    return dict(tokens=tokens, doc_start=doc_start, cotangent=cotangent, norm_in=norm_in, w_in=w_in, w_gates=w_gates, conv_w=conv_w, decay=decay, norm_out=norm_out, w_out=w_out, norm_ffn=norm_ffn, w_up=w_up, w_down=w_down, moment_norm_in=moment_norm_in, moment_w_in=moment_w_in, moment_w_gates=moment_w_gates, moment_conv_w=moment_conv_w, moment_decay=moment_decay, moment_norm_out=moment_norm_out, moment_w_out=moment_w_out, moment_norm_ffn=moment_norm_ffn, moment_w_up=moment_w_up, moment_w_down=moment_w_down)


EPSILON = 1e-06
MOMENTUM = 0.95
RATE = 0.05
RATE_SMALL = 0.3
NEWTON_A = 3.4445
NEWTON_B = -4.775
NEWTON_C = 2.0315
NEWTON_STEPS = 5
HIGHEST_LEVEL = lax.Precision.HIGHEST

def silu(value):
    return value * jax.nn.sigmoid(value)

def rms_unit(value_rows):
    return value_rows * lax.rsqrt(lax.optimization_barrier(jnp.mean(value_rows * value_rows, axis=-1, keepdims=True)) + EPSILON)

def rms_apply(value_rows, gain):
    return rms_unit(value_rows) * gain

def rms_back(value_rows, gain, upstream):
    scale = lax.rsqrt(lax.optimization_barrier(jnp.mean(value_rows * value_rows, axis=-1, keepdims=True)) + EPSILON)
    unit = value_rows * scale
    inner = upstream * gain
    return scale * (inner - unit * lax.optimization_barrier(jnp.mean(inner * unit, axis=-1, keepdims=True)))

def keep_factors(document_start_mask):
    length = document_start_mask.shape[0]
    alive = 1.0 - document_start_mask
    padded = jnp.concatenate([jnp.ones((CONV - 1,), jnp.float32), alive])
    columns = [jnp.ones((length,), jnp.float32)]
    for tap in range(1, CONV):
        columns.append(columns[-1] * padded[CONV - tap:CONV - tap + length])
    return jnp.stack(columns, 1)

def convolve(extended, conv_w, keep):
    length = keep.shape[0]
    total_sum = jnp.zeros((length,) + extended.shape[1:], jnp.float32)
    for tap in range(CONV):
        total_sum = total_sum + conv_w[tap] * extended[CONV - 1 - tap:CONV - 1 - tap + length] * keep[:, tap, None, None]
    return total_sum

def apply_activation(mixed_tokens, output_logits, decay):
    active = silu(mixed_tokens)
    query_rows = active[..., :KEY_SIZE]
    key_rows = active[..., KEY_SIZE:2 * KEY_SIZE]
    value_rows = active[..., 2 * KEY_SIZE:]
    query_rows = query_rows * lax.rsqrt(lax.optimization_barrier(jnp.sum(query_rows * query_rows, axis=-1, keepdims=True)) + EPSILON) * KEY_SIZE ** (-0.5)
    key_rows = key_rows * lax.rsqrt(lax.optimization_barrier(jnp.sum(key_rows * key_rows, axis=-1, keepdims=True)) + EPSILON)
    write_strength = jax.nn.sigmoid(output_logits[:, 1])
    gate_logarithm = -jnp.exp(decay[0]) * jax.nn.softplus(output_logits[:, 0] + decay[1])
    return (query_rows, key_rows, value_rows, write_strength, gate_logarithm)

def block_list(array):
    return jnp.moveaxis(array.reshape((-1, BLOCK_TOKENS) + array.shape[1:]), 2, 0)

def unblocks(array):
    shifted = jnp.moveaxis(array, 0, 2)
    return shifted.reshape((-1,) + shifted.shape[2:])

def block_recurrence(query_rows, key_rows, value_rows, write_strength, gate_logarithm, block_spans, initial_state):
    size = query_rows.shape[2]
    total_sum = jnp.cumsum(gate_logarithm, axis=-1)
    count = jnp.cumsum(block_spans, axis=-1)
    places = jnp.arange(size)
    lower = places[:, None] >= places[None, :]
    strict = (places[:, None] > places[None, :]).astype(jnp.float32)
    same = (count[:, :, None] == count[:, None, :]) & lower
    spread = total_sum[..., :, None] - total_sum[..., None, :]
    decay_mat = jnp.where(same, jnp.exp(jnp.where(same, spread, 0.0)), 0.0)
    head_part = jnp.exp(total_sum) * (count == 0).astype(jnp.float32)
    tail_part = jnp.exp(total_sum[..., -1:] - total_sum) * (count == count[:, -1:]).astype(jnp.float32)
    identity = jnp.eye(size, dtype=jnp.float32)
    keys_beta = key_rows * write_strength[..., None]
    negated = -jnp.einsum('bncd,bnmd->bncm', keys_beta, key_rows, precision=HIGHEST_LEVEL) * decay_mat * strict
    inverse = identity + negated
    power = negated
    for level in range(size.bit_length() - 2):
        power = jnp.einsum('bncm,bnmj->bncj', power, power, precision=HIGHEST_LEVEL)
        inverse = jnp.einsum('bncm,bnmj->bncj', inverse, identity + power, precision=HIGHEST_LEVEL)
    weights = jnp.einsum('bncm,bnmd->bncd', inverse, keys_beta * head_part[..., None], precision=HIGHEST_LEVEL)
    targets = jnp.einsum('bncm,bnmw->bncw', inverse, value_rows * write_strength[..., None], precision=HIGHEST_LEVEL)
    scores = jnp.einsum('bncd,bnmd->bncm', query_rows, key_rows, precision=HIGHEST_LEVEL) * decay_mat

    def leading(array):
        return jnp.moveaxis(array, 1, 0)
    pieces = (leading(query_rows * head_part[..., None]), leading(weights), leading(targets), leading(scores), leading(key_rows * tail_part[..., None]), leading(head_part[..., -1]))

    def advance(state, piece):
        queries, weight, target, score, keyed, last = piece
        fresh_value = target - jnp.einsum('bcd,bdw->bcw', weight, state, precision=HIGHEST_LEVEL)
        result = jnp.einsum('bcd,bdw->bcw', queries, state, precision=HIGHEST_LEVEL) + jnp.einsum('bcm,bmw->bcw', score, fresh_value, precision=HIGHEST_LEVEL)
        state = last[:, None, None] * state + jnp.einsum('bcd,bcw->bdw', keyed, fresh_value, precision=HIGHEST_LEVEL)
        return (state, result)
    final_state, block_results = lax.scan(advance, initial_state, pieces)
    return (jnp.moveaxis(block_results, 0, 1), final_state)

def gated_norm(attended_output, gate_part, norm_out):
    return rms_apply(attended_output, norm_out) * silu(gate_part)

def mixer_whole(conv_in, conv_w, output_logits, decay, gate_part, norm_out, document_start_mask):
    extended = jnp.concatenate([jnp.zeros((CONV - 1,) + conv_in.shape[1:], jnp.float32), conv_in])
    mixed_tokens = convolve(extended, conv_w, keep_factors(document_start_mask))
    query_rows, key_rows, value_rows, write_strength, gate_logarithm = apply_activation(mixed_tokens, output_logits, decay)
    head_count = conv_in.shape[1]
    block_results, final_state = block_recurrence(block_list(query_rows), block_list(key_rows), block_list(value_rows), block_list(write_strength), block_list(gate_logarithm), document_start_mask.reshape(-1, BLOCK_TOKENS), jnp.zeros((head_count, KEY_SIZE, VALUE_SIZE), jnp.float32))
    return gated_norm(unblocks(block_results), gate_part, norm_out)

def rounded(value):
    return lax.optimization_barrier(value.astype(jnp.bfloat16)).astype(jnp.float32)

def orthogonal(look):
    begin = rounded(look)
    total_sum = lax.optimization_barrier(jnp.sum(begin * begin, axis=(1, 2), keepdims=True))
    current = rounded(begin / (jnp.sqrt(total_sum) + 1e-07))
    for turn in range(NEWTON_STEPS):
        gram = rounded(jnp.einsum('bri,brj->bij', current, current, precision=HIGHEST_LEVEL))
        poly = rounded(NEWTON_B * gram + NEWTON_C * jnp.einsum('bij,bjk->bik', gram, gram, precision=HIGHEST_LEVEL))
        current = rounded(NEWTON_A * current + jnp.einsum('bri,bij->brj', current, poly, precision=HIGHEST_LEVEL))
    return current

def muon_scale(width):
    return RATE * 0.2 * math.sqrt(max(D, width))

def reference(tokens, doc_start, cotangent, norm_in, w_in, w_gates, conv_w, decay, norm_out, w_out, norm_ffn, w_up, w_down, moment_norm_in, moment_w_in, moment_w_gates, moment_conv_w, moment_decay, moment_norm_out, moment_w_out, moment_norm_ffn, moment_w_up, moment_w_down):
    document_start_mask = doc_start.astype(jnp.float32)
    in_b = w_in.reshape(D, H * QKVG).astype(jnp.bfloat16)
    gates_b = w_gates.reshape(D, 2 * H).astype(jnp.bfloat16)
    out_b = w_out.reshape(H * VALUE_SIZE, D).astype(jnp.bfloat16)
    up_b = w_up.reshape(D, 2 * FF).astype(jnp.bfloat16)
    down_b = w_down.astype(jnp.bfloat16)
    unit_in = rms_unit(tokens)
    normed_in = (unit_in * norm_in).astype(jnp.bfloat16)
    proj = rounded(jnp.dot(normed_in, in_b, preferred_element_type=jnp.float32)).reshape(TOKENS, H, QKVG)
    output_logits = jnp.dot(normed_in, gates_b, preferred_element_type=jnp.float32).reshape(TOKENS, 2, H)
    conv_in = proj[..., :CONV_CH]
    gate_part = proj[..., CONV_CH:]
    mixer_fn = jax.checkpoint(functools.partial(mixer_whole, document_start_mask=document_start_mask))
    gated, mixer_pull = jax.vjp(mixer_fn, conv_in, conv_w, output_logits, decay, gate_part, norm_out)
    gated_b = gated.astype(jnp.bfloat16).reshape(TOKENS, H * VALUE_SIZE)
    residual = tokens + jnp.dot(gated_b, out_b, preferred_element_type=jnp.float32)
    unit_ffn = rms_unit(residual)
    normed_ffn = (unit_ffn * norm_ffn).astype(jnp.bfloat16)
    ffn_pre = jnp.dot(normed_ffn, up_b, preferred_element_type=jnp.float32).reshape(TOKENS, 2, FF)
    gate_pre = ffn_pre[:, 0]
    lift = ffn_pre[:, 1]
    active = (silu(gate_pre) * lift).astype(jnp.bfloat16)
    output = residual + jnp.dot(active, down_b, preferred_element_type=jnp.float32)
    cot_b = cotangent.astype(jnp.bfloat16)
    grad_w_down = jnp.dot(active.T, cot_b, preferred_element_type=jnp.float32)
    d_active = jnp.dot(cot_b, down_b.T, preferred_element_type=jnp.float32)
    sigma = jax.nn.sigmoid(gate_pre)
    d_gate_pre = d_active * lift * sigma * (1.0 + gate_pre * (1.0 - sigma))
    d_lift = d_active * gate_pre * sigma
    d_ffn_pre = jnp.stack([d_gate_pre, d_lift], 1).astype(jnp.bfloat16).reshape(TOKENS, 2 * FF)
    grad_w_up = jnp.dot(normed_ffn.T, d_ffn_pre, preferred_element_type=jnp.float32).reshape(D, 2, FF)
    d_normed_ffn = jnp.dot(d_ffn_pre, up_b.T, preferred_element_type=jnp.float32)
    grad_norm_ffn = lax.optimization_barrier(jnp.sum(d_normed_ffn * unit_ffn, 0))
    d_residual = cotangent + rms_back(residual, norm_ffn, d_normed_ffn)
    res_b = d_residual.astype(jnp.bfloat16)
    grad_w_out = jnp.dot(gated_b.T, res_b, preferred_element_type=jnp.float32).reshape(H, VALUE_SIZE, D)
    d_gated = jnp.dot(res_b, out_b.T, preferred_element_type=jnp.float32).reshape(TOKENS, H, VALUE_SIZE)
    d_conv_in, grad_conv_w, d_logits, grad_decay, d_gate_part, grad_norm_out = mixer_pull(d_gated)
    d_proj = jnp.concatenate([d_conv_in, d_gate_part], -1).astype(jnp.bfloat16).reshape(TOKENS, H * QKVG)
    d_logits_b = d_logits.astype(jnp.bfloat16).reshape(TOKENS, 2 * H)
    grad_w_in = jnp.dot(normed_in.T, d_proj, preferred_element_type=jnp.float32).reshape(D, H, QKVG)
    grad_w_gates = jnp.dot(normed_in.T, d_logits_b, preferred_element_type=jnp.float32).reshape(D, 2, H)
    d_normed_in = jnp.dot(d_proj, in_b.T, preferred_element_type=jnp.float32) + jnp.dot(d_logits_b, gates_b.T, preferred_element_type=jnp.float32)
    grad_norm_in = lax.optimization_barrier(jnp.sum(d_normed_in * unit_in, 0))
    grad_tokens = d_residual + rms_back(tokens, norm_in, d_normed_in)
    small_scale = RATE_SMALL / math.sqrt(TOKENS)

    def small_update(weight, moment, grad):
        fresh_value = MOMENTUM * moment + grad
        return (weight - small_scale * (grad + MOMENTUM * fresh_value), fresh_value)
    new_norm_in, new_moment_norm_in = small_update(norm_in, moment_norm_in, grad_norm_in)
    new_w_gates, new_moment_w_gates = small_update(w_gates, moment_w_gates, grad_w_gates)
    new_conv_w, new_moment_conv_w = small_update(conv_w, moment_conv_w, grad_conv_w)
    new_decay, new_moment_decay = small_update(decay, moment_decay, grad_decay)
    new_norm_out, new_moment_norm_out = small_update(norm_out, moment_norm_out, grad_norm_out)
    new_norm_ffn, new_moment_norm_ffn = small_update(norm_ffn, moment_norm_ffn, grad_norm_ffn)
    new_moment_w_in = MOMENTUM * moment_w_in + grad_w_in
    look_in = grad_w_in + MOMENTUM * new_moment_w_in
    new_moment_w_out = MOMENTUM * moment_w_out + grad_w_out
    look_out = grad_w_out + MOMENTUM * new_moment_w_out
    new_moment_w_up = MOMENTUM * moment_w_up + grad_w_up
    look_up = grad_w_up + MOMENTUM * new_moment_w_up
    new_moment_w_down = MOMENTUM * moment_w_down + grad_w_down
    look_down = grad_w_down + MOMENTUM * new_moment_w_down
    bounds = ((0, KEY_SIZE), (KEY_SIZE, 2 * KEY_SIZE), (2 * KEY_SIZE, CONV_CH), (CONV_CH, QKVG))
    steps_in = []
    for lower_col, upper_col in bounds:
        units = jnp.moveaxis(look_in[:, :, lower_col:upper_col], 1, 0)
        steps_in.append(jnp.moveaxis(orthogonal(units), 0, 1) * muon_scale(upper_col - lower_col))
    new_w_in = w_in - jnp.concatenate(steps_in, -1)
    new_w_out = w_out - jnp.swapaxes(orthogonal(jnp.swapaxes(look_out, 1, 2)), 1, 2) * muon_scale(VALUE_SIZE)
    groups = FF // FG
    up_units = jnp.transpose(look_up.reshape(D, 2, groups, FG), (1, 2, 0, 3)).reshape(2 * groups, D, FG)
    up_steps = jnp.transpose(orthogonal(up_units).reshape(2, groups, D, FG), (2, 0, 1, 3)).reshape(D, 2, FF)
    new_w_up = w_up - up_steps * muon_scale(FG)
    down_units = jnp.swapaxes(look_down.reshape(groups, FG, D), 1, 2)
    new_w_down = w_down - jnp.swapaxes(orthogonal(down_units), 1, 2).reshape(FF, D) * muon_scale(FG)
    return (output, grad_tokens, grad_norm_in, grad_w_in, grad_w_gates, grad_conv_w, grad_decay, grad_norm_out, grad_w_out, grad_norm_ffn, grad_w_up, grad_w_down, new_norm_in, new_w_in, new_w_gates, new_conv_w, new_decay, new_norm_out, new_w_out, new_norm_ffn, new_w_up, new_w_down, new_moment_norm_in, new_moment_w_in, new_moment_w_gates, new_moment_conv_w, new_moment_decay, new_moment_norm_out, new_moment_w_out, new_moment_norm_ffn, new_moment_w_up, new_moment_w_down)
```

```python
import functools
import math

import jax
import jax.numpy as jnp
from jax import lax
from jax.experimental import pallas as pl
from jax.experimental.pallas import tpu as pltpu
from jax.sharding import PartitionSpec as P

D = 1024
KEY_SIZE = 128
VALUE_SIZE = 256
CONV = 4
BLOCK_TOKENS = 64
FG = 352
QKVG = 768
CONV_CH = 512


EPSILON = 1e-06
MOMENTUM = 0.95
RATE = 0.05
RATE_SMALL = 0.3
NEWTON_A = 3.4445
NEWTON_B = -4.775
NEWTON_C = 2.0315
NEWTON_STEPS = 5
HIGHEST_LEVEL = lax.Precision.HIGHEST


def shifted_2(block, axis, distance):
    devices = range(lax.axis_size(axis))
    route = [(i - distance, i) for i in devices if i - distance in devices]
    return lax.ppermute(block, axis, route)


def silu(value):
    return value * jax.nn.sigmoid(value)


def rms_unit(value_rows):
    return value_rows * lax.rsqrt(
        jnp.mean(value_rows * value_rows, axis=-1, keepdims=True) + EPSILON
    )


def rms_back(value_rows, gain, upstream):
    scale = lax.rsqrt(jnp.mean(value_rows * value_rows, axis=-1, keepdims=True) + EPSILON)
    unit = value_rows * scale
    inner = upstream * gain
    return scale * (inner - unit * jnp.mean(inner * unit, axis=-1, keepdims=True))


def keep_factors(document_start_mask):
    length = document_start_mask.shape[0]
    alive = 1.0 - document_start_mask
    padded = jnp.concatenate([jnp.ones((CONV - 1,), jnp.float32), alive])
    columns = [jnp.ones((length,), jnp.float32)]
    for tap in range(1, CONV):
        columns.append(columns[-1] * padded[CONV - tap : CONV - tap + length])
    return jnp.stack(columns, 1)


def tail_factors(alive):
    length = alive.shape[0]
    factors = [jnp.ones((), jnp.float32)]
    for back in range(1, CONV - 1):
        factors.insert(0, factors[0] * alive[length - back])
    return jnp.stack(factors)


def convolve(extended, conv_w, keep):
    length = keep.shape[0]
    total_sum = jnp.zeros((length,) + extended.shape[1:], jnp.float32)
    for tap in range(CONV):
        total_sum = (
            total_sum
            + conv_w[tap]
            * extended[CONV - 1 - tap : CONV - 1 - tap + length]
            * keep[:, tap, None]
        )
    return total_sum


def strengths(output_logits, decay):
    write_strength = jax.nn.sigmoid(output_logits[:, 1])
    gate_logarithm = -jnp.exp(decay[0]) * jax.nn.softplus(output_logits[:, 0] + decay[1])
    return (write_strength, gate_logarithm)


def dot_of(a, b, left, right):
    return lax.dot_general(
        a,
        b,
        (((left,), (right,)), ((), ())),
        precision=HIGHEST_LEVEL,
        preferred_element_type=jnp.float32,
    )


@jax.custom_vjp
def mm(a, b):
    return dot_of(a, b, 1, 0)


mm.defvjp(
    lambda a, b: (dot_of(a, b, 1, 0), (a, b)),
    lambda kept, g: (dot_of(g, kept[1], 1, 1), dot_of(kept[0], g, 0, 0)),
)


@jax.custom_vjp
def mm_nt(a, b):
    return dot_of(a, b, 1, 1)


mm_nt.defvjp(
    lambda a, b: (dot_of(a, b, 1, 1), (a, b)),
    lambda kept, g: (dot_of(g, kept[1], 1, 0), dot_of(g, kept[0], 0, 0)),
)


@jax.custom_vjp
def mm_tn(a, b):
    return dot_of(a, b, 0, 0)


mm_tn.defvjp(
    lambda a, b: (dot_of(a, b, 0, 0), (a, b)),
    lambda kept, g: (dot_of(kept[1], g, 1, 1), dot_of(kept[0], g, 1, 0)),
)


def cut_rows(array):
    return tuple(
        array[at : at + BLOCK_TOKENS] for at in range(0, array.shape[0], BLOCK_TOKENS)
    )


@jax.custom_vjp
def split_rows(array):
    return cut_rows(array)


split_rows.defvjp(
    lambda array: (cut_rows(array), None), lambda kept, g: (jnp.concatenate(g, 0),)
)


@jax.custom_vjp
def given_inverse(negated, inverse):
    return inverse


def given_inverse_back(inverse, g):
    return (dot_of(dot_of(inverse, g, 0, 0), inverse, 1, 1), jnp.zeros_like(g))


given_inverse.defvjp(lambda negated, inverse: (inverse, inverse), given_inverse_back)


def block_masks(span):
    length = span.shape[0]
    rows = lax.broadcasted_iota(jnp.int32, (length, length), 0)
    cols = lax.broadcasted_iota(jnp.int32, (length, length), 1)
    together = (rows // BLOCK_TOKENS) == (cols // BLOCK_TOKENS)
    lower = jnp.where(together & (rows >= cols), 1.0, 0.0)
    strict = jnp.where(together & (rows > cols), 1.0, 0.0)
    upper = jnp.where(together & (rows < cols), 1.0, 0.0)

    def count(matrix, marks):
        return jnp.dot(
            matrix.astype(jnp.bfloat16),
            marks.astype(jnp.bfloat16),
            preferred_element_type=jnp.float32,
        )

    wide = jnp.broadcast_to(span, (length, KEY_SIZE))
    same = jnp.where(count(lower, span * strict) < 0.5, lower, 0.0)
    head_mask = jnp.where(count(lower, wide) < 0.5, 1.0, 0.0)
    tail_mask = jnp.where(count(upper, wide) < 0.5, 1.0, 0.0)
    whole = jnp.broadcast_to(span, (length, VALUE_SIZE))
    last_masks = [
        jnp.where(jnp.sum(part, axis=0, keepdims=True) < 0.5, 1.0, 0.0) for part in cut_rows(whole)
    ]
    return (lower, strict, upper, same, head_mask, tail_mask, last_masks)


def prepare(masks, mixed_q, mixed_k, mixed_v, beta, glog, saved_inverse):
    lower, strict, upper, same, head_mask, tail_mask, last_masks = masks
    length = mixed_q.shape[0]
    active_q = silu(mixed_q)
    active_k = silu(mixed_k)
    values = silu(mixed_v)
    query = (
        active_q
        * lax.rsqrt(jnp.sum(active_q * active_q, axis=-1, keepdims=True) + EPSILON)
        * KEY_SIZE ** (-0.5)
    )
    keys = active_k * lax.rsqrt(jnp.sum(active_k * active_k, axis=-1, keepdims=True) + EPSILON)
    wide = jnp.broadcast_to(glog, (length, KEY_SIZE))
    whole = jnp.broadcast_to(glog, (length, VALUE_SIZE))
    decay_mat = jnp.exp(mm(lower, glog * strict)) * same
    head_part = jnp.exp(mm(lower, wide)) * head_mask
    tail_part = jnp.exp(mm(upper, wide)) * tail_mask
    lasts = [
        jnp.exp(jnp.sum(part, axis=0, keepdims=True)) * mask
        for part, mask in zip(split_rows(whole), last_masks)
    ]
    keys_beta = keys * beta
    negated = -mm_nt(keys_beta, keys) * decay_mat * strict
    if saved_inverse is None:
        rows = lax.broadcasted_iota(jnp.int32, (length, length), 0)
        cols = lax.broadcasted_iota(jnp.int32, (length, length), 1)
        identity = jnp.where(rows == cols, 1.0, 0.0)
        inverse = identity + negated
        power = negated
        for level in range(BLOCK_TOKENS.bit_length() - 2):
            power = mm(power, power)
            inverse = inverse + mm(inverse, power)
    else:
        inverse = given_inverse(negated, saved_inverse)
    weights = mm(inverse, keys_beta * head_part)
    targets = mm(inverse, values * beta)
    scores = mm_nt(query, keys) * decay_mat
    return (query * head_part, weights, targets, scores, keys * tail_part, lasts, inverse)


def run_core(masks, saved_inverse, mixed_q, mixed_k, mixed_v, beta, glog, state):
    queries, weights, targets, scores, keyed, lasts, unused = prepare(
        masks, mixed_q, mixed_k, mixed_v, beta, glog, saved_inverse
    )
    fresh_values = []
    results = []
    for query, weight, target, key, last in zip(
        split_rows(queries), split_rows(weights), split_rows(targets), split_rows(keyed), lasts
    ):
        fresh = target - mm(weight, state)
        results.append(mm(query, state))
        fresh_values.append(fresh)
        state = last * state + mm_tn(key, fresh)
    attended = jnp.concatenate(results, 0) + mm(scores, jnp.concatenate(fresh_values, 0))
    return (attended, state)


def forward_kernel(head_count, mixed_ref, beta_ref, glog_ref, span_ref, carried_ref, fresh_ref, pair_ref, inverse_ref):
    masks = block_masks(span_ref[...])
    rows = lax.broadcasted_iota(jnp.int32, (KEY_SIZE, KEY_SIZE), 0)
    cols = lax.broadcasted_iota(jnp.int32, (KEY_SIZE, KEY_SIZE), 1)
    for head in range(head_count):
        at = head * CONV_CH
        queries, weights, targets, scores, keyed, lasts, inverse = prepare(
            masks,
            mixed_ref[:, at : at + KEY_SIZE],
            mixed_ref[:, at + KEY_SIZE : at + 2 * KEY_SIZE],
            mixed_ref[:, at + 2 * KEY_SIZE : at + CONV_CH],
            beta_ref[head],
            glog_ref[head],
            None,
        )
        inverse_ref[head] = inverse
        transfer = jnp.where(rows == cols, 1.0, 0.0)
        offset = jnp.zeros((KEY_SIZE, VALUE_SIZE), jnp.float32)
        moved = []
        moved_query = []
        fresh_values = []
        results = []
        for query, weight, target, key, last in zip(
            cut_rows(queries), cut_rows(weights), cut_rows(targets), cut_rows(keyed), lasts
        ):
            lost = -dot_of(weight, transfer, 1, 0)
            fresh = target - dot_of(weight, offset, 1, 0)
            moved_query.append(dot_of(query, transfer, 1, 0))
            results.append(dot_of(query, offset, 1, 0))
            moved.append(lost)
            fresh_values.append(fresh)
            transfer = last[:, :KEY_SIZE] * transfer + dot_of(key, lost, 0, 0)
            offset = last * offset + dot_of(key, fresh, 0, 0)
        carried_ref[:, head * KEY_SIZE : (head + 1) * KEY_SIZE] = jnp.concatenate(
            moved_query, 0
        ) + dot_of(scores, jnp.concatenate(moved, 0), 1, 0)
        fresh_ref[:, head * VALUE_SIZE : (head + 1) * VALUE_SIZE] = jnp.concatenate(
            results, 0
        ) + dot_of(scores, jnp.concatenate(fresh_values, 0), 1, 0)
        pair_ref[head, :, :KEY_SIZE] = transfer.astype(jnp.bfloat16)
        pair_ref[head, :, KEY_SIZE:] = offset.astype(jnp.bfloat16)


def gated_norm(attended, gate_part, norm_out):
    return (
        attended
        * lax.rsqrt(jnp.mean(attended * attended, axis=-1, keepdims=True) + EPSILON)
        * norm_out
        * silu(gate_part)
    )


def carry_kernel(head_count, pair_ref, carried_ref, fresh_ref, gate_ref, norm_ref, attended_ref, gated_ref, state_ref):
    place = lax.axis_index("seq")
    for head in range(head_count):

        def step(at, state):
            return dot_of(
                pair_ref[at, head, :, :KEY_SIZE].astype(jnp.float32), state, 1, 0
            ) + pair_ref[at, head, :, KEY_SIZE:].astype(jnp.float32)

        state = lax.fori_loop(0, place, step, jnp.zeros((KEY_SIZE, VALUE_SIZE), jnp.float32))
        state_ref[head] = state
        part = slice(head * VALUE_SIZE, (head + 1) * VALUE_SIZE)
        attended = fresh_ref[:, part] + dot_of(
            carried_ref[:, head * KEY_SIZE : (head + 1) * KEY_SIZE], state, 1, 0
        )
        attended_ref[:, part] = attended
        gated_ref[:, part] = gated_norm(
            attended, gate_ref[:, part].astype(jnp.float32), norm_ref[...]
        ).astype(jnp.bfloat16)


def gate_back_kernel(head_count, upstream_ref, attended_ref, gate_ref, norm_ref, carried_ref, d_attended_ref, d_gate_ref, gain_ref, local_ref):
    gain_total = jnp.zeros((1, VALUE_SIZE), jnp.float32)
    norm_out = norm_ref[...]
    for head in range(head_count):
        part = slice(head * VALUE_SIZE, (head + 1) * VALUE_SIZE)
        attended = attended_ref[:, part]
        gate = gate_ref[:, part].astype(jnp.float32)
        upstream = upstream_ref[:, part]
        scale = lax.rsqrt(jnp.mean(attended * attended, axis=-1, keepdims=True) + EPSILON)
        unit = attended * scale
        sigma = jax.nn.sigmoid(gate)
        open_gate = gate * sigma
        gain_total = gain_total + jnp.sum(upstream * open_gate * unit, axis=0, keepdims=True)
        inner = upstream * open_gate * norm_out
        d_attended = scale * (inner - unit * jnp.mean(inner * unit, axis=-1, keepdims=True))
        d_gate = upstream * unit * norm_out * sigma * (1.0 + gate * (1.0 - sigma))
        d_attended_ref[:, part] = d_attended
        d_gate_ref[:, part] = d_gate.astype(jnp.bfloat16)
        local_ref[head] = dot_of(
            carried_ref[:, head * KEY_SIZE : (head + 1) * KEY_SIZE], d_attended, 0, 0
        ).astype(jnp.bfloat16)
    gain_ref[...] = gain_total


def back_kernel(head_count, pair_ref, local_ref, d_attended_ref, state_ref, inverse_ref, mixed_ref, beta_ref, glog_ref, span_ref, d_mixed_ref, d_beta_ref, d_glog_ref):
    count = lax.axis_size("seq")
    ahead = count - 1 - lax.axis_index("seq")
    masks = block_masks(span_ref[...])
    for head in range(head_count):

        def step(index, state):
            source = count - 1 - index
            return dot_of(
                pair_ref[source, head, :, :KEY_SIZE].astype(jnp.float32), state, 0, 0
            ) + local_ref[source, head].astype(jnp.float32)

        later = lax.fori_loop(0, ahead, step, jnp.zeros((KEY_SIZE, VALUE_SIZE), jnp.float32))
        at = head * CONV_CH
        unused, pull = jax.vjp(
            functools.partial(run_core, masks, inverse_ref[head]),
            mixed_ref[:, at : at + KEY_SIZE],
            mixed_ref[:, at + KEY_SIZE : at + 2 * KEY_SIZE],
            mixed_ref[:, at + 2 * KEY_SIZE : at + CONV_CH],
            beta_ref[head],
            glog_ref[head],
            state_ref[head],
        )
        d_q, d_k, d_v, d_beta, d_glog, unused_state = pull(
            (d_attended_ref[:, head * VALUE_SIZE : (head + 1) * VALUE_SIZE], later)
        )
        d_mixed_ref[:, at : at + KEY_SIZE] = d_q
        d_mixed_ref[:, at + KEY_SIZE : at + 2 * KEY_SIZE] = d_k
        d_mixed_ref[:, at + 2 * KEY_SIZE : at + CONV_CH] = d_v
        d_beta_ref[head] = d_beta
        d_glog_ref[head] = d_glog


def newton_kernel(batch_ref, out_ref):
    for index in range(batch_ref.shape[0]):
        wide = batch_ref[index].astype(jnp.float32)
        total_sum = jnp.sum(jnp.sum(wide * wide, axis=0, keepdims=True), axis=1, keepdims=True)
        current = (wide / (jnp.sqrt(total_sum) + 1e-07)).astype(jnp.bfloat16)
        for turn in range(NEWTON_STEPS):
            gram = lax.dot_general(
                current, current, (((0,), (0,)), ((), ())), preferred_element_type=jnp.float32
            ).astype(jnp.bfloat16)
            poly = (
                NEWTON_B * gram.astype(jnp.float32)
                + NEWTON_C * jnp.dot(gram, gram, preferred_element_type=jnp.float32)
            ).astype(jnp.bfloat16)
            current = (
                NEWTON_A * current.astype(jnp.float32)
                + jnp.dot(current, poly, preferred_element_type=jnp.float32)
            ).astype(jnp.bfloat16)
        out_ref[index] = current


def call_kernel(body, shapes, name, *operands):
    return pl.pallas_call(
        body,
        out_shape=[jax.ShapeDtypeStruct(shape, kind) for shape, kind in shapes],
        in_specs=[pl.BlockSpec(memory_space=pltpu.VMEM)] * len(operands),
        out_specs=[pl.BlockSpec(memory_space=pltpu.VMEM)] * len(shapes),
        compiler_params=pltpu.CompilerParams(vmem_limit_bytes=48 * 1024 * 1024),
        name=name,
    )(*operands)


def head_total(partial_sum):
    return lax.psum(partial_sum.astype(jnp.bfloat16), "head").astype(jnp.float32)


def per_device(
    tokens,
    doc_start,
    cotangent,
    norm_in,
    w_in,
    w_gates,
    conv_w,
    decay,
    norm_out,
    w_out,
    norm_ffn,
    w_up,
    w_down,
    moment_norm_in,
    moment_w_in,
    moment_w_gates,
    moment_conv_w,
    moment_decay,
    moment_norm_out,
    moment_w_out,
    moment_norm_ffn,
    moment_w_up,
    moment_w_down,
):
    length = tokens.shape[0]
    head_count = w_in.shape[1]
    hidden = w_up.shape[2]
    owners = lax.axis_size("seq")
    in_cols = head_count * QKVG
    gate_cols_count = 2 * head_count
    padding = -gate_cols_count % KEY_SIZE
    full_in = lax.all_gather(
        jnp.concatenate(
            [
                w_in.reshape(-1, in_cols),
                w_gates.reshape(-1, gate_cols_count),
                jnp.zeros((w_in.shape[0], padding), jnp.float32),
            ],
            1,
        ).astype(jnp.bfloat16),
        "seq",
        axis=0,
        tiled=True,
    )
    full_out = lax.all_gather(w_out.astype(jnp.bfloat16), "seq", axis=2, tiled=True)
    full_up = lax.all_gather(w_up.astype(jnp.bfloat16), "seq", axis=0, tiled=True)
    full_down = lax.all_gather(w_down.astype(jnp.bfloat16), "seq", axis=1, tiled=True)
    document_start_mask = doc_start.astype(jnp.float32)
    alive = 1.0 - document_start_mask
    span = document_start_mask[:, None]
    unit_in = rms_unit(tokens)
    normed_in = (unit_in * norm_in).astype(jnp.bfloat16)
    projected = jnp.dot(normed_in, full_in, preferred_element_type=jnp.float32)
    proj = lax.optimization_barrier(projected[:, :in_cols].astype(jnp.bfloat16))
    output_logits = projected[:, in_cols : in_cols + gate_cols_count].reshape(
        length, 2, head_count
    )
    conv_in = jnp.concatenate(
        [proj[:, head * QKVG : head * QKVG + CONV_CH] for head in range(head_count)], 1
    )
    gate_part = jnp.concatenate(
        [proj[:, head * QKVG + CONV_CH : (head + 1) * QKVG] for head in range(head_count)], 1
    )
    edge_scale = tail_factors(alive)
    edge = (conv_in[length - CONV + 1 :].astype(jnp.float32) * edge_scale[:, None]).astype(
        jnp.bfloat16
    )
    before = shifted_2(edge, "seq", 1)
    extended = jnp.concatenate([before, conv_in]).astype(jnp.float32)
    keep = keep_factors(document_start_mask)
    conv_flat = conv_w.reshape(CONV, -1)
    mixed, mixed_pull = jax.vjp(lambda e, w: convolve(e, w, keep), extended, conv_flat)
    (beta, glog), strength_pull = jax.vjp(strengths, output_logits, decay)
    beta_cols = beta.T[:, :, None]
    glog_cols = glog.T[:, :, None]
    wide_f32 = (length, head_count * VALUE_SIZE)
    square = (head_count, KEY_SIZE, VALUE_SIZE)
    carried, fresh, pair, inverse = call_kernel(
        functools.partial(forward_kernel, head_count),
        [
            ((length, head_count * KEY_SIZE), jnp.float32),
            (wide_f32, jnp.float32),
            ((head_count, KEY_SIZE, KEY_SIZE + VALUE_SIZE), jnp.bfloat16),
            ((head_count, length, length), jnp.float32),
        ],
        "delta_forward",
        mixed,
        beta_cols,
        glog_cols,
        span,
    )
    pairs = lax.all_gather(pair, "seq")
    attended, gated_b, incoming = call_kernel(
        functools.partial(carry_kernel, head_count),
        [(wide_f32, jnp.float32), (wide_f32, jnp.bfloat16), (square, jnp.float32)],
        "delta_carry",
        pairs,
        carried,
        fresh,
        gate_part,
        norm_out[None],
    )
    out_flat = full_out.reshape(head_count * VALUE_SIZE, -1)
    residual = tokens + head_total(
        jnp.dot(gated_b, out_flat, preferred_element_type=jnp.float32)
    )
    unit_ffn = rms_unit(residual)
    normed_ffn = (unit_ffn * norm_ffn).astype(jnp.bfloat16)
    ffn_pre = jnp.einsum("td,dgf->tgf", normed_ffn, full_up, preferred_element_type=jnp.float32)
    gate_pre = ffn_pre[:, 0]
    lift = ffn_pre[:, 1]
    active = (silu(gate_pre) * lift).astype(jnp.bfloat16)
    output = residual + head_total(jnp.dot(active, full_down, preferred_element_type=jnp.float32))
    cot_b = cotangent.astype(jnp.bfloat16)
    grad_down_part = jnp.einsum("tf,td->fd", active, cot_b, preferred_element_type=jnp.float32)
    d_active = jnp.einsum("td,fd->tf", cot_b, full_down, preferred_element_type=jnp.float32)
    sigma = jax.nn.sigmoid(gate_pre)
    d_gate_pre = d_active * lift * sigma * (1.0 + gate_pre * (1.0 - sigma))
    d_lift = d_active * gate_pre * sigma
    d_ffn_pre = jnp.stack([d_gate_pre, d_lift], 1).astype(jnp.bfloat16)
    grad_up_part = jnp.einsum(
        "td,tgf->dgf", normed_ffn, d_ffn_pre, preferred_element_type=jnp.float32
    )
    d_ffn_part = jnp.einsum("tgf,dgf->td", d_ffn_pre, full_up, preferred_element_type=jnp.float32)
    gain_ffn_part = jnp.sum(d_ffn_part * unit_ffn, 0)
    d_residual = cotangent + rms_back(residual, norm_ffn, head_total(d_ffn_part))
    res_b = d_residual.astype(jnp.bfloat16)
    grad_out_part = jnp.einsum("tv,td->vd", gated_b, res_b, preferred_element_type=jnp.float32)
    d_gated = jnp.einsum("td,vd->tv", res_b, out_flat, preferred_element_type=jnp.float32)
    d_attended, d_gate_part, gain_out_row, local_gradient = call_kernel(
        functools.partial(gate_back_kernel, head_count),
        [
            (wide_f32, jnp.float32),
            (wide_f32, jnp.bfloat16),
            ((1, VALUE_SIZE), jnp.float32),
            (square, jnp.bfloat16),
        ],
        "gate_back",
        d_gated,
        attended,
        gate_part,
        norm_out[None],
        carried,
    )
    gain_out_part = gain_out_row[0]
    local_gradients = lax.all_gather(local_gradient, "seq")
    d_mixed, d_beta, d_glog = call_kernel(
        functools.partial(back_kernel, head_count),
        [
            (mixed.shape, jnp.float32),
            (beta_cols.shape, jnp.float32),
            (beta_cols.shape, jnp.float32),
        ],
        "delta_back",
        pairs,
        local_gradients,
        d_attended,
        incoming,
        inverse,
        mixed,
        beta_cols,
        glog_cols,
        span,
    )
    d_extended, grad_conv_flat = mixed_pull(d_mixed)
    grad_conv_part = grad_conv_flat.reshape(conv_w.shape)
    d_logits, grad_decay_part = strength_pull((d_beta[:, :, 0].T, d_glog[:, :, 0].T))
    returned_edge = shifted_2(d_extended[: CONV - 1], "seq", -1)
    inner = d_extended[CONV - 1 :]
    d_conv_in = jnp.concatenate(
        [
            inner[: length - CONV + 1],
            inner[length - CONV + 1 :] + returned_edge * edge_scale[:, None],
        ]
    ).astype(jnp.bfloat16)
    columns = []
    for head in range(head_count):
        columns.append(d_conv_in[:, head * CONV_CH : (head + 1) * CONV_CH])
        columns.append(d_gate_part[:, head * VALUE_SIZE : (head + 1) * VALUE_SIZE])
    columns.append(d_logits.reshape(length, gate_cols_count).astype(jnp.bfloat16))
    columns.append(jnp.zeros((length, padding), jnp.bfloat16))
    d_proj = jnp.concatenate(columns, 1)
    grad_in_part = jnp.einsum("td,tc->dc", normed_in, d_proj, preferred_element_type=jnp.float32)
    d_in_part = jnp.einsum("tc,dc->td", d_proj, full_in, preferred_element_type=jnp.float32)
    gain_in_part = jnp.sum(d_in_part * unit_in, 0)
    grad_tokens = d_residual + rms_back(tokens, norm_in, head_total(d_in_part))
    grad_in_rows = lax.psum_scatter(
        grad_in_part.astype(jnp.bfloat16), "seq", scatter_dimension=0, tiled=True
    ).astype(jnp.float32)
    grad_w_in = grad_in_rows[:, :in_cols].reshape(w_in.shape)
    grad_w_gates = grad_in_rows[:, in_cols : in_cols + gate_cols_count].reshape(w_gates.shape)
    grad_w_out, grad_w_up, grad_w_down = (
        lax.psum_scatter(
            grad_out_part.reshape(head_count, VALUE_SIZE, -1).astype(jnp.bfloat16),
            "seq",
            scatter_dimension=2,
            tiled=True,
        ).astype(jnp.float32),
        lax.psum_scatter(
            grad_up_part.astype(jnp.bfloat16), "seq", scatter_dimension=0, tiled=True
        ).astype(jnp.float32),
        lax.psum_scatter(
            grad_down_part.astype(jnp.bfloat16), "seq", scatter_dimension=1, tiled=True
        ).astype(jnp.float32),
    )
    grad_conv_w, grad_decay = lax.psum((grad_conv_part, grad_decay_part), "seq")
    grad_norm_in, grad_norm_out, grad_norm_ffn = lax.psum(
        (gain_in_part, gain_out_part, gain_ffn_part), ("seq", "head")
    )
    small_scale = RATE_SMALL / math.sqrt(length * owners)

    def small_update(weight, moment, grad):
        fresh_moment = MOMENTUM * moment + grad
        return (weight - small_scale * (grad + MOMENTUM * fresh_moment), fresh_moment)

    new_norm_in, new_moment_norm_in = small_update(norm_in, moment_norm_in, grad_norm_in)
    new_w_gates, new_moment_w_gates = small_update(w_gates, moment_w_gates, grad_w_gates)
    new_conv_w, new_moment_conv_w = small_update(conv_w, moment_conv_w, grad_conv_w)
    new_decay, new_moment_decay = small_update(decay, moment_decay, grad_decay)
    new_norm_out, new_moment_norm_out = small_update(norm_out, moment_norm_out, grad_norm_out)
    new_norm_ffn, new_moment_norm_ffn = small_update(norm_ffn, moment_norm_ffn, grad_norm_ffn)
    new_moment_w_in = MOMENTUM * moment_w_in + grad_w_in
    look_in = grad_w_in + MOMENTUM * new_moment_w_in
    new_moment_w_out = MOMENTUM * moment_w_out + grad_w_out
    look_out = grad_w_out + MOMENTUM * new_moment_w_out
    new_moment_w_up = MOMENTUM * moment_w_up + grad_w_up
    look_up = grad_w_up + MOMENTUM * new_moment_w_up
    new_moment_w_down = MOMENTUM * moment_w_down + grad_w_down
    look_down = grad_w_down + MOMENTUM * new_moment_w_down
    bounds = ((0, KEY_SIZE), (KEY_SIZE, 2 * KEY_SIZE), (2 * KEY_SIZE, CONV_CH), (CONV_CH, QKVG))
    pieces = []
    widths = []
    for head in range(head_count):
        for lower_col, upper_col in bounds:
            pieces.append(look_in[:, head, lower_col:upper_col])
            widths.append(upper_col - lower_col)
        pieces.append(look_out[head].T)
        widths.append(VALUE_SIZE)
    groups = hidden // FG
    for group in range(groups):
        pieces.append(look_up[:, 0, group * FG : (group + 1) * FG])
        pieces.append(look_up[:, 1, group * FG : (group + 1) * FG])
        pieces.append(look_down[group * FG : (group + 1) * FG].T)
        widths.extend([FG, FG, FG])
    rounded_pieces = [piece.astype(jnp.bfloat16) for piece in pieces]
    count = len(rounded_pieces)
    rows = rounded_pieces[0].shape[0]
    widest = max(widths)
    per_owner = -(-count // owners)
    padded = [jnp.pad(piece, ((0, 0), (0, widest - piece.shape[1]))) for piece in rounded_pieces]
    padded = padded + [jnp.zeros((rows, widest), jnp.bfloat16)] * (owners * per_owner - count)
    outgoing = jnp.stack(padded).reshape(owners, per_owner, rows, widest)
    arrived = lax.all_to_all(outgoing, "seq", split_axis=0, concat_axis=2, tiled=True)[0]
    finished = call_kernel(newton_kernel, [(arrived.shape, jnp.bfloat16)], "newton", arrived)[0][
        None
    ]
    returned = lax.all_to_all(finished, "seq", split_axis=2, concat_axis=0, tiled=True)
    flat = returned.reshape(owners * per_owner, rows, widest)
    orthos = [flat[index, :, : widths[index]] for index in range(count)]
    updates = [
        orthos[index].astype(jnp.float32) * (RATE * 0.2 * math.sqrt(max(D, widths[index])))
        for index in range(count)
    ]
    cursor = 0
    in_heads = []
    out_heads = []
    for head in range(head_count):
        in_heads.append(jnp.concatenate(updates[cursor : cursor + 4], -1))
        out_heads.append(updates[cursor + 4].T)
        cursor += 5
    gate_cols = []
    lift_cols = []
    down_rows = []
    for group in range(groups):
        gate_cols.append(updates[cursor])
        lift_cols.append(updates[cursor + 1])
        down_rows.append(updates[cursor + 2].T)
        cursor += 3
    new_w_in = w_in - jnp.stack(in_heads, 1)
    new_w_out = w_out - jnp.stack(out_heads, 0)
    new_w_up = w_up - jnp.stack([jnp.concatenate(gate_cols, -1), jnp.concatenate(lift_cols, -1)], 1)
    new_w_down = w_down - jnp.concatenate(down_rows, 0)
    return (
        output,
        grad_tokens,
        grad_norm_in,
        grad_w_in,
        grad_w_gates,
        grad_conv_w,
        grad_decay,
        grad_norm_out,
        grad_w_out,
        grad_norm_ffn,
        grad_w_up,
        grad_w_down,
        new_norm_in,
        new_w_in,
        new_w_gates,
        new_conv_w,
        new_decay,
        new_norm_out,
        new_w_out,
        new_norm_ffn,
        new_w_up,
        new_w_down,
        new_moment_norm_in,
        new_moment_w_in,
        new_moment_w_gates,
        new_moment_conv_w,
        new_moment_decay,
        new_moment_norm_out,
        new_moment_w_out,
        new_moment_norm_ffn,
        new_moment_w_up,
        new_moment_w_down,
    )


def solution(mesh):
    return jax.shard_map(
        per_device,
        mesh=mesh,
        in_specs=(
            P("seq", None),
            P("seq"),
            P("seq", None),
            P(),
            P("seq", "head", None),
            P("seq", None, "head"),
            P(None, "head", None),
            P(None, "head"),
            P(),
            P("head", None, "seq"),
            P(),
            P("seq", None, "head"),
            P("head", "seq"),
            P(),
            P("seq", "head", None),
            P("seq", None, "head"),
            P(None, "head", None),
            P(None, "head"),
            P(),
            P("head", None, "seq"),
            P(),
            P("seq", None, "head"),
            P("head", "seq"),
        ),
        out_specs=(
            P("seq", None),
            P("seq", None),
            P(),
            P("seq", "head", None),
            P("seq", None, "head"),
            P(None, "head", None),
            P(None, "head"),
            P(),
            P("head", None, "seq"),
            P(),
            P("seq", None, "head"),
            P("head", "seq"),
            P(),
            P("seq", "head", None),
            P("seq", None, "head"),
            P(None, "head", None),
            P(None, "head"),
            P(),
            P("head", None, "seq"),
            P(),
            P("seq", None, "head"),
            P("head", "seq"),
            P(),
            P("seq", "head", None),
            P("seq", None, "head"),
            P(None, "head", None),
            P(None, "head"),
            P(),
            P("head", None, "seq"),
            P(),
            P("seq", None, "head"),
            P("head", "seq"),
        ),
        check_vma=False,
    )
```

```python
import functools
import math

import jax
import jax.numpy as jnp
from jax import lax
from jax.experimental import pallas as pl
from jax.experimental.pallas import tpu as pltpu
from jax.sharding import PartitionSpec as P

D = 1024
KEY_SIZE = 128
VALUE_SIZE = 256
CONV = 4
BLOCK_TOKENS = 64
FG = 352
QKVG = 768
CONV_CH = 512


EPSILON = 1e-06
MOMENTUM = 0.95
RATE = 0.05
RATE_SMALL = 0.3
NEWTON_A = 3.4445
NEWTON_B = -4.775
NEWTON_C = 2.0315
NEWTON_STEPS = 5
HIGHEST_LEVEL = lax.Precision.HIGHEST


def shifted_2(block, axis, distance):
    devices = range(lax.axis_size(axis))
    route = [(i - distance, i) for i in devices if i - distance in devices]
    return lax.ppermute(block, axis, route)


def silu(value):
    return value * jax.nn.sigmoid(value)


def rms_unit(value_rows):
    return value_rows * lax.rsqrt(
        jnp.mean(value_rows * value_rows, axis=-1, keepdims=True) + EPSILON
    )


def rms_back(value_rows, gain, upstream):
    scale = lax.rsqrt(jnp.mean(value_rows * value_rows, axis=-1, keepdims=True) + EPSILON)
    unit = value_rows * scale
    inner = upstream * gain
    return scale * (inner - unit * jnp.mean(inner * unit, axis=-1, keepdims=True))


def keep_factors(document_start_mask):
    length = document_start_mask.shape[0]
    alive = 1.0 - document_start_mask
    padded = jnp.concatenate([jnp.ones((CONV - 1,), jnp.float32), alive])
    columns = [jnp.ones((length,), jnp.float32)]
    for tap in range(1, CONV):
        columns.append(columns[-1] * padded[CONV - tap : CONV - tap + length])
    return jnp.stack(columns, 1)


def tail_factors(alive):
    length = alive.shape[0]
    factors = [jnp.ones((), jnp.float32)]
    for back in range(1, CONV - 1):
        factors.insert(0, factors[0] * alive[length - back])
    return jnp.stack(factors)


def convolve(extended, conv_w, keep):
    length = keep.shape[0]
    total_sum = jnp.zeros((length,) + extended.shape[1:], jnp.float32)
    for tap in range(CONV):
        total_sum = (
            total_sum
            + conv_w[tap]
            * extended[CONV - 1 - tap : CONV - 1 - tap + length]
            * keep[:, tap, None]
        )
    return total_sum


def strengths(output_logits, decay):
    write_strength = jax.nn.sigmoid(output_logits[:, 1])
    gate_logarithm = -jnp.exp(decay[0]) * jax.nn.softplus(output_logits[:, 0] + decay[1])
    return (write_strength, gate_logarithm)


def dot_of(a, b, left, right):
    return lax.dot_general(
        a,
        b,
        (((left,), (right,)), ((), ())),
        precision=HIGHEST_LEVEL,
        preferred_element_type=jnp.float32,
    )


@jax.custom_vjp
def mm(a, b):
    return dot_of(a, b, 1, 0)


mm.defvjp(
    lambda a, b: (dot_of(a, b, 1, 0), (a, b)),
    lambda kept, g: (dot_of(g, kept[1], 1, 1), dot_of(kept[0], g, 0, 0)),
)


@jax.custom_vjp
def mm_nt(a, b):
    return dot_of(a, b, 1, 1)


mm_nt.defvjp(
    lambda a, b: (dot_of(a, b, 1, 1), (a, b)),
    lambda kept, g: (dot_of(g, kept[1], 1, 0), dot_of(g, kept[0], 0, 0)),
)


@jax.custom_vjp
def mm_tn(a, b):
    return dot_of(a, b, 0, 0)


mm_tn.defvjp(
    lambda a, b: (dot_of(a, b, 0, 0), (a, b)),
    lambda kept, g: (dot_of(kept[1], g, 1, 1), dot_of(kept[0], g, 1, 0)),
)


def cut_rows(array):
    return tuple(
        array[at : at + BLOCK_TOKENS] for at in range(0, array.shape[0], BLOCK_TOKENS)
    )


@jax.custom_vjp
def split_rows(array):
    return cut_rows(array)


split_rows.defvjp(
    lambda array: (cut_rows(array), None), lambda kept, g: (jnp.concatenate(g, 0),)
)


@jax.custom_vjp
def given_inverse(negated, inverse):
    return inverse


def given_inverse_back(inverse, g):
    return (dot_of(dot_of(inverse, g, 0, 0), inverse, 1, 1), jnp.zeros_like(g))


given_inverse.defvjp(lambda negated, inverse: (inverse, inverse), given_inverse_back)


def block_masks(span):
    length = span.shape[0]
    rows = lax.broadcasted_iota(jnp.int32, (length, length), 0)
    cols = lax.broadcasted_iota(jnp.int32, (length, length), 1)
    together = (rows // BLOCK_TOKENS) == (cols // BLOCK_TOKENS)
    lower = jnp.where(together & (rows >= cols), 1.0, 0.0)
    strict = jnp.where(together & (rows > cols), 1.0, 0.0)
    upper = jnp.where(together & (rows < cols), 1.0, 0.0)

    def count(matrix, marks):
        return jnp.dot(
            matrix.astype(jnp.bfloat16),
            marks.astype(jnp.bfloat16),
            preferred_element_type=jnp.float32,
        )

    wide = jnp.broadcast_to(span, (length, KEY_SIZE))
    same = jnp.where(count(lower, span * strict) < 0.5, lower, 0.0)
    head_mask = jnp.where(count(lower, wide) < 0.5, 1.0, 0.0)
    tail_mask = jnp.where(count(upper, wide) < 0.5, 1.0, 0.0)
    whole = jnp.broadcast_to(span, (length, VALUE_SIZE))
    last_masks = [
        jnp.where(jnp.sum(part, axis=0, keepdims=True) < 0.5, 1.0, 0.0) for part in cut_rows(whole)
    ]
    return (lower, strict, upper, same, head_mask, tail_mask, last_masks)


def prepare(masks, mixed_q, mixed_k, mixed_v, beta, glog, saved_inverse):
    lower, strict, upper, same, head_mask, tail_mask, last_masks = masks
    length = mixed_q.shape[0]
    active_q = silu(mixed_q)
    active_k = silu(mixed_k)
    values = silu(mixed_v)
    query = (
        active_q
        * lax.rsqrt(jnp.sum(active_q * active_q, axis=-1, keepdims=True) + EPSILON)
        * KEY_SIZE ** (-0.5)
    )
    keys = active_k * lax.rsqrt(jnp.sum(active_k * active_k, axis=-1, keepdims=True) + EPSILON)
    wide = jnp.broadcast_to(glog, (length, KEY_SIZE))
    whole = jnp.broadcast_to(glog, (length, VALUE_SIZE))
    decay_mat = jnp.exp(mm(lower, glog * strict)) * same
    head_part = jnp.exp(mm(lower, wide)) * head_mask
    tail_part = jnp.exp(mm(upper, wide)) * tail_mask
    lasts = [
        jnp.exp(jnp.sum(part, axis=0, keepdims=True)) * mask
        for part, mask in zip(split_rows(whole), last_masks)
    ]
    keys_beta = keys * beta
    negated = -mm_nt(keys_beta, keys) * decay_mat * strict
    if saved_inverse is None:
        rows = lax.broadcasted_iota(jnp.int32, (length, length), 0)
        cols = lax.broadcasted_iota(jnp.int32, (length, length), 1)
        identity = jnp.where(rows == cols, 1.0, 0.0)
        inverse = identity + negated
        power = negated
        for level in range(BLOCK_TOKENS.bit_length() - 2):
            power = mm(power, power)
            inverse = inverse + mm(inverse, power)
    else:
        inverse = given_inverse(negated, saved_inverse)
    weights = mm(inverse, keys_beta * head_part)
    targets = mm(inverse, values * beta)
    scores = mm_nt(query, keys) * decay_mat
    return (query * head_part, weights, targets, scores, keys * tail_part, lasts, inverse)


def run_core(masks, saved_inverse, mixed_q, mixed_k, mixed_v, beta, glog, state):
    queries, weights, targets, scores, keyed, lasts, unused = prepare(
        masks, mixed_q, mixed_k, mixed_v, beta, glog, saved_inverse
    )
    fresh_values = []
    results = []
    for query, weight, target, key, last in zip(
        split_rows(queries), split_rows(weights), split_rows(targets), split_rows(keyed), lasts
    ):
        fresh = target - mm(weight, state)
        results.append(mm(query, state))
        fresh_values.append(fresh)
        state = last * state + mm_tn(key, fresh)
    attended = jnp.concatenate(results, 0) + mm(scores, jnp.concatenate(fresh_values, 0))
    return (attended, state)


def forward_kernel(head_count, mixed_ref, beta_ref, glog_ref, span_ref, carried_ref, fresh_ref, pair_ref, inverse_ref):
    masks = block_masks(span_ref[...])
    rows = lax.broadcasted_iota(jnp.int32, (KEY_SIZE, KEY_SIZE), 0)
    cols = lax.broadcasted_iota(jnp.int32, (KEY_SIZE, KEY_SIZE), 1)
    for head in range(head_count):
        at = head * CONV_CH
        queries, weights, targets, scores, keyed, lasts, inverse = prepare(
            masks,
            mixed_ref[:, at : at + KEY_SIZE],
            mixed_ref[:, at + KEY_SIZE : at + 2 * KEY_SIZE],
            mixed_ref[:, at + 2 * KEY_SIZE : at + CONV_CH],
            beta_ref[head],
            glog_ref[head],
            None,
        )
        inverse_ref[head] = inverse
        transfer = jnp.where(rows == cols, 1.0, 0.0)
        offset = jnp.zeros((KEY_SIZE, VALUE_SIZE), jnp.float32)
        moved = []
        moved_query = []
        fresh_values = []
        results = []
        for query, weight, target, key, last in zip(
            cut_rows(queries), cut_rows(weights), cut_rows(targets), cut_rows(keyed), lasts
        ):
            lost = -dot_of(weight, transfer, 1, 0)
            fresh = target - dot_of(weight, offset, 1, 0)
            moved_query.append(dot_of(query, transfer, 1, 0))
            results.append(dot_of(query, offset, 1, 0))
            moved.append(lost)
            fresh_values.append(fresh)
            transfer = last[:, :KEY_SIZE] * transfer + dot_of(key, lost, 0, 0)
            offset = last * offset + dot_of(key, fresh, 0, 0)
        carried_ref[:, head * KEY_SIZE : (head + 1) * KEY_SIZE] = jnp.concatenate(
            moved_query, 0
        ) + dot_of(scores, jnp.concatenate(moved, 0), 1, 0)
        fresh_ref[:, head * VALUE_SIZE : (head + 1) * VALUE_SIZE] = jnp.concatenate(
            results, 0
        ) + dot_of(scores, jnp.concatenate(fresh_values, 0), 1, 0)
        pair_ref[head, :, :KEY_SIZE] = transfer.astype(jnp.bfloat16)
        pair_ref[head, :, KEY_SIZE:] = offset.astype(jnp.bfloat16)


def gated_norm(attended, gate_part, norm_out):
    return (
        attended
        * lax.rsqrt(jnp.mean(attended * attended, axis=-1, keepdims=True) + EPSILON)
        * norm_out
        * silu(gate_part)
    )


def carry_kernel(head_count, pair_ref, carried_ref, fresh_ref, gate_ref, norm_ref, attended_ref, gated_ref, state_ref):
    place = lax.axis_index("seq")
    for head in range(head_count):

        def step(at, state):
            return dot_of(
                pair_ref[at, head, :, :KEY_SIZE].astype(jnp.float32), state, 1, 0
            ) + pair_ref[at, head, :, KEY_SIZE:].astype(jnp.float32)

        state = lax.fori_loop(0, place, step, jnp.zeros((KEY_SIZE, VALUE_SIZE), jnp.float32))
        state_ref[head] = state
        part = slice(head * VALUE_SIZE, (head + 1) * VALUE_SIZE)
        attended = fresh_ref[:, part] + dot_of(
            carried_ref[:, head * KEY_SIZE : (head + 1) * KEY_SIZE], state, 1, 0
        )
        attended_ref[:, part] = attended
        gated_ref[:, part] = gated_norm(
            attended, gate_ref[:, part].astype(jnp.float32), norm_ref[...]
        ).astype(jnp.bfloat16)


def gate_back_kernel(head_count, upstream_ref, attended_ref, gate_ref, norm_ref, carried_ref, d_attended_ref, d_gate_ref, gain_ref, local_ref):
    gain_total = jnp.zeros((1, VALUE_SIZE), jnp.float32)
    norm_out = norm_ref[...]
    for head in range(head_count):
        part = slice(head * VALUE_SIZE, (head + 1) * VALUE_SIZE)
        attended = attended_ref[:, part]
        gate = gate_ref[:, part].astype(jnp.float32)
        upstream = upstream_ref[:, part]
        scale = lax.rsqrt(jnp.mean(attended * attended, axis=-1, keepdims=True) + EPSILON)
        unit = attended * scale
        sigma = jax.nn.sigmoid(gate)
        open_gate = gate * sigma
        gain_total = gain_total + jnp.sum(upstream * open_gate * unit, axis=0, keepdims=True)
        inner = upstream * open_gate * norm_out
        d_attended = scale * (inner - unit * jnp.mean(inner * unit, axis=-1, keepdims=True))
        d_gate = upstream * unit * norm_out * sigma * (1.0 + gate * (1.0 - sigma))
        d_attended_ref[:, part] = d_attended
        d_gate_ref[:, part] = d_gate.astype(jnp.bfloat16)
        local_ref[head] = dot_of(
            carried_ref[:, head * KEY_SIZE : (head + 1) * KEY_SIZE], d_attended, 0, 0
        ).astype(jnp.bfloat16)
    gain_ref[...] = gain_total


def back_kernel(head_count, pair_ref, local_ref, d_attended_ref, state_ref, inverse_ref, mixed_ref, beta_ref, glog_ref, span_ref, d_mixed_ref, d_beta_ref, d_glog_ref):
    count = lax.axis_size("seq")
    ahead = count - 1 - lax.axis_index("seq")
    masks = block_masks(span_ref[...])
    for head in range(head_count):

        def step(index, state):
            source = count - 1 - index
            return dot_of(
                pair_ref[source, head, :, :KEY_SIZE].astype(jnp.float32), state, 0, 0
            ) + local_ref[source, head].astype(jnp.float32)

        later = lax.fori_loop(0, ahead, step, jnp.zeros((KEY_SIZE, VALUE_SIZE), jnp.float32))
        at = head * CONV_CH
        unused, pull = jax.vjp(
            functools.partial(run_core, masks, inverse_ref[head]),
            mixed_ref[:, at : at + KEY_SIZE],
            mixed_ref[:, at + KEY_SIZE : at + 2 * KEY_SIZE],
            mixed_ref[:, at + 2 * KEY_SIZE : at + CONV_CH],
            beta_ref[head],
            glog_ref[head],
            state_ref[head],
        )
        d_q, d_k, d_v, d_beta, d_glog, unused_state = pull(
            (d_attended_ref[:, head * VALUE_SIZE : (head + 1) * VALUE_SIZE], later)
        )
        d_mixed_ref[:, at : at + KEY_SIZE] = d_q
        d_mixed_ref[:, at + KEY_SIZE : at + 2 * KEY_SIZE] = d_k
        d_mixed_ref[:, at + 2 * KEY_SIZE : at + CONV_CH] = d_v
        d_beta_ref[head] = d_beta
        d_glog_ref[head] = d_glog


def newton_kernel(batch_ref, out_ref):
    for index in range(batch_ref.shape[0]):
        wide = batch_ref[index].astype(jnp.float32)
        total_sum = jnp.sum(jnp.sum(wide * wide, axis=0, keepdims=True), axis=1, keepdims=True)
        current = (wide / (jnp.sqrt(total_sum) + 1e-07)).astype(jnp.bfloat16)
        for turn in range(NEWTON_STEPS):
            gram = lax.dot_general(
                current, current, (((0,), (0,)), ((), ())), preferred_element_type=jnp.float32
            ).astype(jnp.bfloat16)
            poly = (
                NEWTON_B * gram.astype(jnp.float32)
                + NEWTON_C * jnp.dot(gram, gram, preferred_element_type=jnp.float32)
            ).astype(jnp.bfloat16)
            current = (
                NEWTON_A * current.astype(jnp.float32)
                + jnp.dot(current, poly, preferred_element_type=jnp.float32)
            ).astype(jnp.bfloat16)
        out_ref[index] = current


def call_kernel(body, shapes, name, *operands):
    return pl.pallas_call(
        body,
        out_shape=[jax.ShapeDtypeStruct(shape, kind) for shape, kind in shapes],
        in_specs=[pl.BlockSpec(memory_space=pltpu.VMEM)] * len(operands),
        out_specs=[pl.BlockSpec(memory_space=pltpu.VMEM)] * len(shapes),
        compiler_params=pltpu.CompilerParams(vmem_limit_bytes=48 * 1024 * 1024),
        name=name,
    )(*operands)


def head_total(partial_sum):
    return lax.psum(partial_sum.astype(jnp.bfloat16), "head").astype(jnp.float32)


def per_device(
    tokens,
    doc_start,
    cotangent,
    norm_in,
    w_in,
    w_gates,
    conv_w,
    decay,
    norm_out,
    w_out,
    norm_ffn,
    w_up,
    w_down,
    moment_norm_in,
    moment_w_in,
    moment_w_gates,
    moment_conv_w,
    moment_decay,
    moment_norm_out,
    moment_w_out,
    moment_norm_ffn,
    moment_w_up,
    moment_w_down,
):
    length = tokens.shape[0]
    head_count = w_in.shape[1]
    hidden = w_up.shape[2]
    owners = lax.axis_size("seq")
    in_cols = head_count * QKVG
    gate_cols_count = 2 * head_count
    padding = -gate_cols_count % KEY_SIZE
    full_in = lax.all_gather(
        jnp.concatenate(
            [
                w_in.reshape(-1, in_cols),
                w_gates.reshape(-1, gate_cols_count),
                jnp.zeros((w_in.shape[0], padding), jnp.float32),
            ],
            1,
        ).astype(jnp.bfloat16),
        "seq",
        axis=0,
        tiled=True,
    )
    full_out = lax.all_gather(w_out.astype(jnp.bfloat16), "seq", axis=2, tiled=True)
    full_up = lax.all_gather(w_up.astype(jnp.bfloat16), "seq", axis=0, tiled=True)
    full_down = lax.all_gather(w_down.astype(jnp.bfloat16), "seq", axis=1, tiled=True)
    document_start_mask = doc_start.astype(jnp.float32)
    alive = 1.0 - document_start_mask
    span = document_start_mask[:, None]
    unit_in = rms_unit(tokens)
    normed_in = (unit_in * norm_in).astype(jnp.bfloat16)
    projected = jnp.dot(normed_in, full_in, preferred_element_type=jnp.float32)
    proj = lax.optimization_barrier(projected[:, :in_cols].astype(jnp.bfloat16))
    output_logits = projected[:, in_cols : in_cols + gate_cols_count].reshape(
        length, 2, head_count
    )
    conv_in = jnp.concatenate(
        [proj[:, head * QKVG : head * QKVG + CONV_CH] for head in range(head_count)], 1
    )
    gate_part = jnp.concatenate(
        [proj[:, head * QKVG + CONV_CH : (head + 1) * QKVG] for head in range(head_count)], 1
    )
    edge_scale = tail_factors(alive)
    edge = (conv_in[length - CONV + 1 :].astype(jnp.float32) * edge_scale[:, None]).astype(
        jnp.bfloat16
    )
    before = shifted_2(edge, "seq", 1)
    extended = jnp.concatenate([before, conv_in]).astype(jnp.float32)
    keep = keep_factors(document_start_mask)
    conv_flat = conv_w.reshape(CONV, -1)
    mixed, mixed_pull = jax.vjp(lambda e, w: convolve(e, w, keep), extended, conv_flat)
    (beta, glog), strength_pull = jax.vjp(strengths, output_logits, decay)
    beta_cols = beta.T[:, :, None]
    glog_cols = glog.T[:, :, None]
    wide_f32 = (length, head_count * VALUE_SIZE)
    square = (head_count, KEY_SIZE, VALUE_SIZE)
    carried, fresh, pair, inverse = call_kernel(
        functools.partial(forward_kernel, head_count),
        [
            ((length, head_count * KEY_SIZE), jnp.float32),
            (wide_f32, jnp.float32),
            ((head_count, KEY_SIZE, KEY_SIZE + VALUE_SIZE), jnp.bfloat16),
            ((head_count, length, length), jnp.float32),
        ],
        "delta_forward",
        mixed,
        beta_cols,
        glog_cols,
        span,
    )
    pairs = lax.all_gather(pair, "seq")
    attended, gated_b, incoming = call_kernel(
        functools.partial(carry_kernel, head_count),
        [(wide_f32, jnp.float32), (wide_f32, jnp.bfloat16), (square, jnp.float32)],
        "delta_carry",
        pairs,
        carried,
        fresh,
        gate_part,
        norm_out[None],
    )
    out_flat = full_out.reshape(head_count * VALUE_SIZE, -1)
    residual = tokens + head_total(
        jnp.dot(gated_b, out_flat, preferred_element_type=jnp.float32)
    )
    unit_ffn = rms_unit(residual)
    normed_ffn = (unit_ffn * norm_ffn).astype(jnp.bfloat16)
    ffn_pre = jnp.einsum("td,dgf->tgf", normed_ffn, full_up, preferred_element_type=jnp.float32)
    gate_pre = ffn_pre[:, 0]
    lift = ffn_pre[:, 1]
    active = (silu(gate_pre) * lift).astype(jnp.bfloat16)
    output = residual + head_total(jnp.dot(active, full_down, preferred_element_type=jnp.float32))
    cot_b = cotangent.astype(jnp.bfloat16)
    grad_down_part = jnp.einsum("tf,td->fd", active, cot_b, preferred_element_type=jnp.float32)
    d_active = jnp.einsum("td,fd->tf", cot_b, full_down, preferred_element_type=jnp.float32)
    sigma = jax.nn.sigmoid(gate_pre)
    d_gate_pre = d_active * lift * sigma * (1.0 + gate_pre * (1.0 - sigma))
    d_lift = d_active * gate_pre * sigma
    d_ffn_pre = jnp.stack([d_gate_pre, d_lift], 1).astype(jnp.bfloat16)
    grad_up_part = jnp.einsum(
        "td,tgf->dgf", normed_ffn, d_ffn_pre, preferred_element_type=jnp.float32
    )
    d_ffn_part = jnp.einsum("tgf,dgf->td", d_ffn_pre, full_up, preferred_element_type=jnp.float32)
    gain_ffn_part = jnp.sum(d_ffn_part * unit_ffn, 0)
    d_residual = cotangent + rms_back(residual, norm_ffn, head_total(d_ffn_part))
    res_b = d_residual.astype(jnp.bfloat16)
    grad_out_part = jnp.einsum("tv,td->vd", gated_b, res_b, preferred_element_type=jnp.float32)
    d_gated = jnp.einsum("td,vd->tv", res_b, out_flat, preferred_element_type=jnp.float32)
    d_attended, d_gate_part, gain_out_row, local_gradient = call_kernel(
        functools.partial(gate_back_kernel, head_count),
        [
            (wide_f32, jnp.float32),
            (wide_f32, jnp.bfloat16),
            ((1, VALUE_SIZE), jnp.float32),
            (square, jnp.bfloat16),
        ],
        "gate_back",
        d_gated,
        attended,
        gate_part,
        norm_out[None],
        carried,
    )
    gain_out_part = gain_out_row[0]
    local_gradients = lax.all_gather(local_gradient, "seq")
    d_mixed, d_beta, d_glog = call_kernel(
        functools.partial(back_kernel, head_count),
        [
            (mixed.shape, jnp.float32),
            (beta_cols.shape, jnp.float32),
            (beta_cols.shape, jnp.float32),
        ],
        "delta_back",
        pairs,
        local_gradients,
        d_attended,
        incoming,
        inverse,
        mixed,
        beta_cols,
        glog_cols,
        span,
    )
    d_extended, grad_conv_flat = mixed_pull(d_mixed)
    grad_conv_part = grad_conv_flat.reshape(conv_w.shape)
    d_logits, grad_decay_part = strength_pull((d_beta[:, :, 0].T, d_glog[:, :, 0].T))
    returned_edge = shifted_2(d_extended[: CONV - 1], "seq", -1)
    inner = d_extended[CONV - 1 :]
    d_conv_in = jnp.concatenate(
        [
            inner[: length - CONV + 1],
            inner[length - CONV + 1 :] + returned_edge * edge_scale[:, None],
        ]
    ).astype(jnp.bfloat16)
    columns = []
    for head in range(head_count):
        columns.append(d_conv_in[:, head * CONV_CH : (head + 1) * CONV_CH])
        columns.append(d_gate_part[:, head * VALUE_SIZE : (head + 1) * VALUE_SIZE])
    columns.append(d_logits.reshape(length, gate_cols_count).astype(jnp.bfloat16))
    columns.append(jnp.zeros((length, padding), jnp.bfloat16))
    d_proj = jnp.concatenate(columns, 1)
    grad_in_part = jnp.einsum("td,tc->dc", normed_in, d_proj, preferred_element_type=jnp.float32)
    d_in_part = jnp.einsum("tc,dc->td", d_proj, full_in, preferred_element_type=jnp.float32)
    gain_in_part = jnp.sum(d_in_part * unit_in, 0)
    grad_tokens = d_residual + rms_back(tokens, norm_in, head_total(d_in_part))
    grad_in_rows = lax.psum_scatter(
        grad_in_part.astype(jnp.bfloat16), "seq", scatter_dimension=0, tiled=True
    ).astype(jnp.float32)
    grad_w_in = grad_in_rows[:, :in_cols].reshape(w_in.shape)
    grad_w_gates = grad_in_rows[:, in_cols : in_cols + gate_cols_count].reshape(w_gates.shape)
    grad_w_out, grad_w_up, grad_w_down = (
        lax.psum_scatter(
            grad_out_part.reshape(head_count, VALUE_SIZE, -1).astype(jnp.bfloat16),
            "seq",
            scatter_dimension=2,
            tiled=True,
        ).astype(jnp.float32),
        lax.psum_scatter(
            grad_up_part.astype(jnp.bfloat16), "seq", scatter_dimension=0, tiled=True
        ).astype(jnp.float32),
        lax.psum_scatter(
            grad_down_part.astype(jnp.bfloat16), "seq", scatter_dimension=1, tiled=True
        ).astype(jnp.float32),
    )
    gain_sizes = (gain_in_part.shape[0], gain_out_part.shape[0], gain_ffn_part.shape[0])
    gain_sums = jnp.sum(
        lax.all_gather(
            jnp.concatenate([gain_in_part, gain_out_part, gain_ffn_part]), ("seq", "head")
        ),
        0,
    )
    grad_norm_in = gain_sums[: gain_sizes[0]]
    grad_norm_out = gain_sums[gain_sizes[0] : gain_sizes[0] + gain_sizes[1]]
    grad_norm_ffn = gain_sums[gain_sizes[0] + gain_sizes[1] :]
    taps_size = grad_conv_part.size
    tap_sums = jnp.sum(
        lax.all_gather(
            jnp.concatenate(
                [
                    grad_conv_part.reshape(-1),
                    grad_decay_part.reshape(-1),
                    jnp.zeros((KEY_SIZE - grad_decay_part.size,), jnp.float32),
                ]
            ),
            "seq",
        ),
        0,
    )
    grad_conv_w = tap_sums[:taps_size].reshape(conv_w.shape)
    grad_decay = tap_sums[taps_size : taps_size + grad_decay_part.size].reshape(decay.shape)
    small_scale = RATE_SMALL / math.sqrt(length * owners)

    def small_update(weight, moment, grad):
        fresh_moment = MOMENTUM * moment + grad
        return (weight - small_scale * (grad + MOMENTUM * fresh_moment), fresh_moment)

    new_norm_in, new_moment_norm_in = small_update(norm_in, moment_norm_in, grad_norm_in)
    new_w_gates, new_moment_w_gates = small_update(w_gates, moment_w_gates, grad_w_gates)
    new_conv_w, new_moment_conv_w = small_update(conv_w, moment_conv_w, grad_conv_w)
    new_decay, new_moment_decay = small_update(decay, moment_decay, grad_decay)
    new_norm_out, new_moment_norm_out = small_update(norm_out, moment_norm_out, grad_norm_out)
    new_norm_ffn, new_moment_norm_ffn = small_update(norm_ffn, moment_norm_ffn, grad_norm_ffn)
    new_moment_w_in = MOMENTUM * moment_w_in + grad_w_in
    look_in = grad_w_in + MOMENTUM * new_moment_w_in
    new_moment_w_out = MOMENTUM * moment_w_out + grad_w_out
    look_out = grad_w_out + MOMENTUM * new_moment_w_out
    new_moment_w_up = MOMENTUM * moment_w_up + grad_w_up
    look_up = grad_w_up + MOMENTUM * new_moment_w_up
    new_moment_w_down = MOMENTUM * moment_w_down + grad_w_down
    look_down = grad_w_down + MOMENTUM * new_moment_w_down
    bounds = ((0, KEY_SIZE), (KEY_SIZE, 2 * KEY_SIZE), (2 * KEY_SIZE, CONV_CH), (CONV_CH, QKVG))
    pieces = []
    widths = []
    for head in range(head_count):
        for lower_col, upper_col in bounds:
            pieces.append(look_in[:, head, lower_col:upper_col])
            widths.append(upper_col - lower_col)
        pieces.append(look_out[head].T)
        widths.append(VALUE_SIZE)
    groups = hidden // FG
    for group in range(groups):
        pieces.append(look_up[:, 0, group * FG : (group + 1) * FG])
        pieces.append(look_up[:, 1, group * FG : (group + 1) * FG])
        pieces.append(look_down[group * FG : (group + 1) * FG].T)
        widths.extend([FG, FG, FG])
    rounded_pieces = [piece.astype(jnp.bfloat16) for piece in pieces]
    count = len(rounded_pieces)
    rows = rounded_pieces[0].shape[0]
    widest = max(widths)
    per_owner = -(-count // owners)
    padded = [jnp.pad(piece, ((0, 0), (0, widest - piece.shape[1]))) for piece in rounded_pieces]
    padded = padded + [jnp.zeros((rows, widest), jnp.bfloat16)] * (owners * per_owner - count)
    outgoing = jnp.stack(padded).reshape(owners, per_owner, rows, widest)
    arrived = lax.all_to_all(outgoing, "seq", split_axis=0, concat_axis=2, tiled=True)[0]
    finished = call_kernel(newton_kernel, [(arrived.shape, jnp.bfloat16)], "newton", arrived)[0][
        None
    ]
    returned = lax.all_to_all(finished, "seq", split_axis=2, concat_axis=0, tiled=True)
    flat = returned.reshape(owners * per_owner, rows, widest)
    orthos = [flat[index, :, : widths[index]] for index in range(count)]
    updates = [
        orthos[index].astype(jnp.float32) * (RATE * 0.2 * math.sqrt(max(D, widths[index])))
        for index in range(count)
    ]
    cursor = 0
    in_heads = []
    out_heads = []
    for head in range(head_count):
        in_heads.append(jnp.concatenate(updates[cursor : cursor + 4], -1))
        out_heads.append(updates[cursor + 4].T)
        cursor += 5
    gate_cols = []
    lift_cols = []
    down_rows = []
    for group in range(groups):
        gate_cols.append(updates[cursor])
        lift_cols.append(updates[cursor + 1])
        down_rows.append(updates[cursor + 2].T)
        cursor += 3
    new_w_in = w_in - jnp.stack(in_heads, 1)
    new_w_out = w_out - jnp.stack(out_heads, 0)
    new_w_up = w_up - jnp.stack([jnp.concatenate(gate_cols, -1), jnp.concatenate(lift_cols, -1)], 1)
    new_w_down = w_down - jnp.concatenate(down_rows, 0)
    return (
        output,
        grad_tokens,
        grad_norm_in,
        grad_w_in,
        grad_w_gates,
        grad_conv_w,
        grad_decay,
        grad_norm_out,
        grad_w_out,
        grad_norm_ffn,
        grad_w_up,
        grad_w_down,
        new_norm_in,
        new_w_in,
        new_w_gates,
        new_conv_w,
        new_decay,
        new_norm_out,
        new_w_out,
        new_norm_ffn,
        new_w_up,
        new_w_down,
        new_moment_norm_in,
        new_moment_w_in,
        new_moment_w_gates,
        new_moment_conv_w,
        new_moment_decay,
        new_moment_norm_out,
        new_moment_w_out,
        new_moment_norm_ffn,
        new_moment_w_up,
        new_moment_w_down,
    )


def solution(mesh):
    return jax.shard_map(
        per_device,
        mesh=mesh,
        in_specs=(
            P("seq", None),
            P("seq"),
            P("seq", None),
            P(),
            P("seq", "head", None),
            P("seq", None, "head"),
            P(None, "head", None),
            P(None, "head"),
            P(),
            P("head", None, "seq"),
            P(),
            P("seq", None, "head"),
            P("head", "seq"),
            P(),
            P("seq", "head", None),
            P("seq", None, "head"),
            P(None, "head", None),
            P(None, "head"),
            P(),
            P("head", None, "seq"),
            P(),
            P("seq", None, "head"),
            P("head", "seq"),
        ),
        out_specs=(
            P("seq", None),
            P("seq", None),
            P(),
            P("seq", "head", None),
            P("seq", None, "head"),
            P(None, "head", None),
            P(None, "head"),
            P(),
            P("head", None, "seq"),
            P(),
            P("seq", None, "head"),
            P("head", "seq"),
            P(),
            P("seq", "head", None),
            P("seq", None, "head"),
            P(None, "head", None),
            P(None, "head"),
            P(),
            P("head", None, "seq"),
            P(),
            P("seq", None, "head"),
            P("head", "seq"),
            P(),
            P("seq", "head", None),
            P("seq", None, "head"),
            P(None, "head", None),
            P(None, "head"),
            P(),
            P("head", None, "seq"),
            P(),
            P("seq", None, "head"),
            P("head", "seq"),
        ),
        check_vma=False,
    )
```
